32 devices in a mesh: ctx: 8 (over z, y), head: 4 (over x, core).
Axes of the slice: x: 2, y: 2, z: 4, core: 2. Of those that a mesh axis runs over, the one named last changes fastest.
Arguments:
- norm_out: bfloat16 [1152, 4096], P('ctx'), may hold values from -1.75 to 1.75
- out_grad: bfloat16 [1152, 512], P('ctx', 'head'), may hold values from -6 to 6
- attn_out: bfloat16 [1152, 512], P('ctx', 'head'), may hold values from -12 to 12
- log_norm: float32 [4, 1152], P('head', 'ctx'), may hold values from 5.5 to 7.5
- query_weight: bfloat16 [4096, 512], P(None, 'head'), may hold values from -0.09375 to 0.09375
- key_weight: bfloat16 [4096, 128], P(None, 'head'), may hold values from -0.09375 to 0.09375
- value_weight: bfloat16 [4096, 128], P(None, 'head'), may hold values from -0.09375 to 0.09375
- span_order: int32 [16], replicated, may hold values from 0 to 15, each once
Outputs:
- input_grad: bfloat16 [1152, 4096], P(('ctx', 'head'))
The draws below stay inside these ranges and needn't reach their ends.
Inputs may be any that keep to these rules, and one draw needn't show every extreme that they name: Shard c holds block span_order[2 c] in its first 72 rows and span_order[2 c + 1] in the rest; each of the 16 blocks once.
All inputs are finite; a program needn't handle non-finite values.
Results may differ from the reference program's by a relative error of at most 0.015.
Values may be sent and summed in bfloat16 or wider, within the bound.
No kernel may reach another device: no remote copies, remote signals or barrier semaphores. Data moves between devices by JAX's collectives and lax.ppermute only.
A program may use at most 64 MiB of HBM per device.

```python
import jax
import jax.numpy as jnp
from jax import lax

D = 4096
HD = 128
GROUP = 4
STEPS = 3
TOK_DEV = 144
QH = 4
KVH = 1
TOKENS = 1152
HALF = 72
SPANS = 16
N_CTX = 8


def draw_norm_out(key, part):
    values = jax.random.uniform(key, (TOKENS, D), jnp.float32, -1.75, 1.75)
    return values.astype(jnp.bfloat16)


def block_levels(stream_key, dims, split, low, largest):
    def one(dim, blocks):
        heights = jax.random.uniform(jax.random.fold_in(jax.random.fold_in(stream_key, 6), dim), (blocks,), jnp.float32, low / len(split), largest / len(split))
        return jnp.repeat(jnp.exp(heights), dims[dim] // blocks).reshape((-1,) + (1,) * (len(dims) - dim - 1))

    factor_of = one(*split[0])
    for cut in split[1:]:
        factor_of = factor_of * one(*cut)
    return factor_of


def noise(key, shape, scale, reach, cuts=(), kind=jnp.bfloat16):
    level = block_levels(key, shape, cuts, -0.22, 0.18) if cuts else 1.0
    array = jax.random.normal(key, shape, jnp.float32) * scale * level
    return jnp.minimum(jnp.maximum(array, -reach), reach).astype(kind)


def setup_inputs(seed: int = 0) -> dict:
    splits = jax.random.split(jax.random.key(seed), 9)
    norm_out = draw_norm_out(jax.random.fold_in(splits[8], 71), 0)
    out_grad = noise(splits[1], (TOKENS, QH * HD), 1.0, 6.0, ((0, 8), (1, 4)))
    attn_out = noise(splits[2], (TOKENS, QH * HD), 2.0, 12.0, ((0, 8), (1, 4)))
    log_norm = jnp.clip(5.5 + 2.0 * jax.random.uniform(splits[3], (QH, TOKENS), jnp.float32) ** block_levels(splits[3], (QH, TOKENS), ((0, 4), (1, 8)), -0.2, 0.2), 5.5, 7.5)
    query_weight = noise(splits[4], (D, QH * HD), D ** -0.5, 0.09375, ((1, 4),))
    key_weight = noise(splits[5], (D, KVH * HD), D ** -0.5, 0.09375, ((1, 4),))
    value_weight = noise(splits[6], (D, KVH * HD), D ** -0.5, 0.09375, ((1, 4),))
    span_order = jax.random.permutation(splits[7], SPANS).astype(jnp.int32)
    return {"norm_out": norm_out, "out_grad": out_grad, "attn_out": attn_out, "log_norm": log_norm, "query_weight": query_weight, "key_weight": key_weight, "value_weight": value_weight, "span_order": span_order}


def positions(span_order):
    rows = jnp.arange(TOKENS, dtype=jnp.int32)
    shard = rows // TOK_DEV
    local = rows % TOK_DEV
    span = span_order[2 * shard + local // HALF]
    return (span * HALF + local % HALF).astype(jnp.int32)


def head_grads(query, key_g, value_g, grad_o, attn_o, lse, pos):
    scale = HD ** -0.5
    qs = query.reshape(N_CTX, TOK_DEV, HD)
    ks = key_g.reshape(N_CTX, TOK_DEV, HD)
    vs = value_g.reshape(N_CTX, TOK_DEV, HD)
    gs = grad_o.reshape(N_CTX, TOK_DEV, HD)
    delta = jnp.sum(grad_o.astype(jnp.float32) * attn_o.astype(jnp.float32), axis=1).reshape(N_CTX, TOK_DEV)
    lses = lse.reshape(N_CTX, TOK_DEV)
    ps = pos.reshape(N_CTX, TOK_DEV)

    def per_shard(shard):
        sources = [(shard - step) % N_CTX for step in range(STEPS + 1)]
        kcat = jnp.concatenate([ks[src] for src in sources], axis=0)
        vcat = jnp.concatenate([vs[src] for src in sources], axis=0)
        kpos = jnp.concatenate([ps[src] for src in sources], axis=0)
        qrow = qs[shard]
        grow = gs[shard]
        scores = jnp.dot(qrow, kcat.T, preferred_element_type=jnp.float32) * scale
        allowed = kpos[None, :] <= ps[shard][:, None]
        prob = jnp.where(allowed, jnp.exp(scores - lses[shard][:, None]), jnp.float32(0.0))
        dprob = jnp.dot(grow, vcat.T, preferred_element_type=jnp.float32)
        dscore = prob * (dprob - delta[shard][:, None])
        prob_b = prob.astype(jnp.bfloat16)
        dscore_b = dscore.astype(jnp.bfloat16)
        dquery = jnp.dot(dscore_b, kcat, preferred_element_type=jnp.float32) * scale
        dkey = jnp.dot(dscore_b.T, qrow, preferred_element_type=jnp.float32) * scale
        dvalue = jnp.dot(prob_b.T, grow, preferred_element_type=jnp.float32)
        return dquery, dkey.reshape(STEPS + 1, TOK_DEV, HD), dvalue.reshape(STEPS + 1, TOK_DEV, HD)

    dquery, dkey, dvalue = lax.map(per_shard, jnp.arange(N_CTX, dtype=jnp.int32))
    key_total = jnp.zeros((N_CTX, TOK_DEV, HD), jnp.float32)
    value_total = jnp.zeros((N_CTX, TOK_DEV, HD), jnp.float32)
    for step in range(STEPS + 1):
        key_total = key_total + jnp.roll(dkey[:, step], -step, axis=0)
        value_total = value_total + jnp.roll(dvalue[:, step], -step, axis=0)
    return dquery.reshape(TOKENS, HD), key_total.reshape(TOKENS, HD), value_total.reshape(TOKENS, HD)


def reference(norm_out, out_grad, attn_out, log_norm, query_weight, key_weight, value_weight, span_order):
    pos = positions(span_order)
    quarter = HD // GROUP
    result = jnp.zeros((TOKENS, D), jnp.float32)
    for group in range(KVH):
        gcols = slice(group * HD, (group + 1) * HD)
        key_g = jnp.dot(norm_out, key_weight[:, gcols], preferred_element_type=jnp.float32).astype(jnp.bfloat16)
        value_g = jnp.dot(norm_out, value_weight[:, gcols], preferred_element_type=jnp.float32).astype(jnp.bfloat16)
        key_sum = jnp.zeros((TOKENS, HD), jnp.float32)
        value_sum = jnp.zeros((TOKENS, HD), jnp.float32)
        dquery_list = []
        for member in range(GROUP):
            head_num = group * GROUP + member
            cols = slice(head_num * HD, (head_num + 1) * HD)
            query = jnp.dot(norm_out, query_weight[:, cols], preferred_element_type=jnp.float32).astype(jnp.bfloat16)
            dquery, dkey, dvalue = head_grads(query, key_g, value_g, out_grad[:, cols], attn_out[:, cols], log_norm[head_num], pos)
            key_sum = key_sum + dkey
            value_sum = value_sum + dvalue
            dquery_list.append(dquery.astype(jnp.bfloat16))
        key_b = key_sum.astype(jnp.bfloat16)
        value_b = value_sum.astype(jnp.bfloat16)
        for member in range(GROUP):
            head_num = group * GROUP + member
            cols = slice(head_num * HD, (head_num + 1) * HD)
            inner = slice(member * quarter, (member + 1) * quarter)
            wcols = slice(group * HD + member * quarter, group * HD + (member + 1) * quarter)
            term = jnp.dot(dquery_list[member], query_weight[:, cols].T, preferred_element_type=jnp.float32)
            term = term + jnp.dot(key_b[:, inner], key_weight[:, wcols].T, preferred_element_type=jnp.float32)
            term = term + jnp.dot(value_b[:, inner], value_weight[:, wcols].T, preferred_element_type=jnp.float32)
            term_b = lax.optimization_barrier(term.astype(jnp.bfloat16))
            result = result + term_b.astype(jnp.float32)
    return result.astype(jnp.bfloat16)
```

```python
import functools

import jax
import jax.numpy as jnp
from jax import lax
from jax.experimental import pallas as pl
from jax.experimental.pallas import tpu as pltpu
from jax.sharding import PartitionSpec as P

GROUP = 4
STEPS = 3
EXTRA = 16
F32 = jnp.float32
BF16 = jnp.bfloat16


def nn(left, right):
    return jnp.dot(left, right, preferred_element_type=F32)


def nt(left, right):
    return lax.dot_general(left, right, (((1,), (1,)), ((), ())), preferred_element_type=F32)


def tn(left, right):
    return lax.dot_general(left, right, (((0,), (0,)), ((), ())), preferred_element_type=F32)


def three_pieces(row):
    high = row.astype(BF16).astype(F32)
    rest = row - high
    middle = rest.astype(BF16).astype(F32)
    return high, middle, rest - middle


def project_kernel(
    norm_ref, wq_ref, kw_ref, vw_ref, kw2_ref, vw2_ref, grad_ref, attn_ref, lse_ref,
    pack_ref, far_ref, acc_q, acc_b,
):
    step = pl.program_id(0)
    rows = norm_ref.shape[0]
    width = wq_ref.shape[1]
    odd = lax.axis_index("ctx") % 2 == 1

    @pl.when(step == 0)
    def _():
        acc_q[...] = jnp.zeros_like(acc_q)
        acc_b[...] = jnp.zeros_like(acc_b)

    norm = norm_ref[...]
    acc_q[...] += nn(norm, wq_ref[...])
    pair = jnp.concatenate([kw_ref[...], vw_ref[...], kw2_ref[...], vw2_ref[...]], axis=0)
    acc_b[...] += nt(norm, pair)

    @pl.when(step == pl.num_programs(0) - 1)
    def _():
        grad = grad_ref[...]
        query = acc_q[...].astype(BF16)
        keyval = acc_b[...].astype(BF16)
        prod = grad.astype(F32) * attn_ref[...].astype(F32)
        high = prod.astype(BF16)
        low = (prod - high.astype(F32)).astype(BF16)
        ones = jnp.ones((8, width), BF16)
        delta = (nt(ones, high) + nt(ones, low))[0:1, :]
        index = lax.broadcasted_iota(jnp.int32, (EXTRA, rows), 0)
        extra = jnp.zeros((EXTRA, rows), F32)
        for at, piece in enumerate(three_pieces(lse_ref[...]) + three_pieces(delta)):
            extra = jnp.where(index == at, piece, extra)
        extra = extra.astype(BF16)
        pack_ref[0:rows, 0:width] = query
        pack_ref[0:rows, width : 2 * width] = grad
        pack_ref[0:rows, 2 * width :] = keyval
        pack_ref[rows:, :] = jnp.zeros((EXTRA, 3 * width), BF16)
        pack_ref[rows:, 0:rows] = extra

        @pl.when(odd)
        def _():
            far_ref[0:rows, 0:width] = keyval
            far_ref[0:rows, width:] = keyval
            far_ref[rows:, :] = jnp.zeros((EXTRA, 2 * width), BF16)

        @pl.when(jnp.logical_not(odd))
        def _():
            far_ref[0:rows, 0:width] = query
            far_ref[0:rows, width:] = grad
            far_ref[rows:, :] = jnp.zeros((EXTRA, 2 * width), BF16)
            far_ref[rows:, 0:rows] = extra


def project(norm_out, query_weight, kw, vw, kw2, vw2, out_grad, attn_out, log_norm):
    rows, depth = norm_out.shape
    width = query_weight.shape[1]
    quarter = kw.shape[0]
    cut = depth // 4
    whole = lambda shape: pl.BlockSpec(shape, lambda k: (0, 0))
    cols = lambda n: pl.BlockSpec((n, cut), lambda k: (0, k))
    return pl.pallas_call(
        project_kernel,
        grid=(depth // cut,),
        out_shape=(
            jax.ShapeDtypeStruct((rows + EXTRA, 3 * width), BF16),
            jax.ShapeDtypeStruct((rows + EXTRA, 2 * width), BF16),
        ),
        in_specs=[
            cols(rows),
            pl.BlockSpec((cut, width), lambda k: (k, 0)),
            cols(quarter),
            cols(quarter),
            cols(quarter),
            cols(quarter),
            whole((rows, width)),
            whole((rows, width)),
            whole((1, rows)),
        ],
        out_specs=(whole((rows + EXTRA, 3 * width)), whole((rows + EXTRA, 2 * width))),
        scratch_shapes=[pltpu.VMEM((rows, width), F32), pltpu.VMEM((rows, width), F32)],
        name="project",
    )(norm_out, query_weight, kw, vw, kw2, vw2, out_grad, attn_out, log_norm)


def attention_kernel(span_ref, pack_ref, near_ref, far_ref, later_ref, kva_ref, kvx_ref, out_ref):
    padded = pack_ref.shape[0]
    rows = padded - EXTRA
    half = rows // 2
    width = kva_ref.shape[1]
    quarter = width // GROUP
    scale = width ** (-0.5)
    shards = lax.axis_size("ctx")
    here = lax.axis_index("ctx")
    odd = here % 2 == 1
    member = lax.axis_index("head") % GROUP

    source = lax.broadcasted_iota(jnp.int32, (width, 2 * width), 0)
    target = lax.broadcasted_iota(jnp.int32, (width, 2 * width), 1)
    place = ((source // quarter) ^ member) * (2 * quarter) + source % quarter
    put_key = jnp.where(target == place, F32(1.0), F32(0.0)).astype(BF16)
    put_value = jnp.where(target == place + quarter, F32(1.0), F32(0.0)).astype(BF16)

    def positions(shard, axis):
        shape = (rows, 1) if axis == 0 else (1, rows)
        index = lax.broadcasted_iota(jnp.int32, shape, axis)
        first = span_ref[2 * shard]
        second = span_ref[2 * shard + 1]
        return jnp.where(index < half, first * half + index, (second - 1) * half + index)

    def queries(block, shard):
        spread = nn(block[0:rows, 0:width], put_key).astype(BF16)
        grad = nn(block[0:rows, width : 2 * width], put_value).astype(BF16)
        tail = block[rows : rows + 8, :].astype(F32)
        lse = tail[0:1, 0:rows] + tail[1:2, 0:rows] + tail[2:3, 0:rows]
        delta = tail[3:4, 0:rows] + tail[4:5, 0:rows] + tail[5:6, 0:rows]
        return spread, grad, lse, delta, positions(shard, 1)

    def keys(at, shard):
        part = slice(at * rows, (at + 1) * rows)
        return jnp.concatenate([kva_ref[part, :], kvx_ref[part, :]], axis=1), positions(shard, 0)

    def block(query, key):
        spread, grad, lse, delta, query_pos = query
        keyval, key_pos = key
        scores = nt(keyval, spread) * scale
        prob = jnp.where(key_pos <= query_pos, jnp.exp(scores - lse), F32(0.0))
        dscore = prob * (nt(keyval, grad) - delta)
        return prob.astype(BF16), dscore.astype(BF16)

    def ring(shard):
        return (shard + 2 * shards) % shards

    before = ring(here - 2)
    after = ring(here + 2)
    flip = 1 - 2 * (here % 2)
    own_query = queries(pack_ref[:, 0 : 2 * width], here)
    own_key = keys(0, here)

    prob, dscore = block(own_query, own_key)
    dquery = tn(dscore, own_key[0])
    dkey = nn(dscore, own_query[0])
    dvalue = nn(prob, own_query[1])
    for at, shard in (
        (1, before),
        (2, ring(before + flip)),
        (3, ring(jnp.where(odd, here - 1, here - 3))),
    ):
        key = keys(at, shard)
        _, dscore = block(own_query, key)
        dquery += tn(dscore, key[0])
    third = jnp.where(odd, far_ref[...], near_ref[:, 0 : 2 * width])
    for packed, shard in (
        (later_ref[0:padded, :], after),
        (later_ref[padded:, :], ring(after + flip)),
        (third, ring(jnp.where(odd, here + 3, here + 1))),
    ):
        query = queries(packed, shard)
        prob, dscore = block(query, own_key)
        dkey += nn(dscore, query[0])
        dvalue += nn(prob, query[1])
    dquery_b = (dquery * scale).astype(BF16)
    out_ref[:, 0:width] = nt(dquery_b, put_key).astype(BF16)
    out_ref[:, width:] = (dkey * scale + dvalue).astype(BF16)


def attention(span_order, pack, near, far, later, kva, kvx):
    rows = pack.shape[0] - EXTRA
    width = kva.shape[1]
    vmem = pl.BlockSpec(memory_space=pltpu.VMEM)
    return pl.pallas_call(
        attention_kernel,
        out_shape=jax.ShapeDtypeStruct((rows, 3 * width), BF16),
        in_specs=[pl.BlockSpec(memory_space=pltpu.SMEM)] + [vmem] * 6,
        out_specs=vmem,
        name="attention",
    )(span_order, pack, near, far, later, kva, kvx)


def split_kernel(mine, grads_ref, send_ref, keep_ref):
    rows, columns = grads_ref.shape
    width = columns // 3
    padded = send_ref.shape[0] // 2
    member = lax.axis_index("head")
    grads = grads_ref[...]
    slot = lax.broadcasted_iota(jnp.int32, (padded, rows), 0)
    token = lax.broadcasted_iota(jnp.int32, (padded, rows), 1)

    def rows_of(owner):
        chosen = jnp.where((token == owner * mine + slot) & (slot < mine), F32(1.0), F32(0.0))
        return nn(chosen.astype(BF16), grads)

    for at, (other, kept) in enumerate(((3, 2), (1, 0))):
        part = slice(at * padded, (at + 1) * padded)
        keep_ref[part, :] = rows_of(member ^ kept).astype(BF16)
        sent = rows_of(member ^ other)
        send_ref[part, 0:width] = sent[:, 0:width].astype(BF16)
        for step in (1, 2):
            lanes = slice(step * width, (step + 1) * width)
            send_ref[part, lanes] = pltpu.roll(sent[:, lanes], width // 2, 1).astype(BF16)


def split_rows(grads, mine):
    padded = -(-mine // 8) * 8
    shape = jax.ShapeDtypeStruct((2 * padded, grads.shape[1]), BF16)
    vmem = pl.BlockSpec(memory_space=pltpu.VMEM)
    return pl.pallas_call(
        functools.partial(split_kernel, mine),
        out_shape=(shape, shape),
        in_specs=[vmem],
        out_specs=(vmem, vmem),
        name="split",
    )(grads)


def term_kernel(width, keep_ref, got_ref, wq_ref, wq2_ref, *refs):
    weights, out_ref = refs[:-1], refs[-1]
    keep = keep_ref[...]
    got = got_ref[...]
    both = keep[:, width:].astype(F32) + got[:, width:].astype(F32)
    total = nt(keep[:, 0:width], wq_ref[...]) + nt(got[:, 0:width], wq2_ref[...])
    stacked = jnp.concatenate([w[...] for w in weights], axis=0)
    total = total + nn(both.astype(BF16), stacked)
    out_ref[...] = total[0 : out_ref.shape[0], :].astype(out_ref.dtype)


def term(at, mine, keep, got, wq, wq2, weights, kind):
    padded = keep.shape[0] // 2
    depth, width = wq.shape
    cut = depth // 4
    part = pl.BlockSpec((padded, keep.shape[1]), lambda k: (at, 0))
    return pl.pallas_call(
        functools.partial(term_kernel, width),
        grid=(depth // cut,),
        out_shape=jax.ShapeDtypeStruct((mine, depth), kind),
        in_specs=[part, part]
        + [pl.BlockSpec((cut, width), lambda k: (k, 0))] * 2
        + [pl.BlockSpec((w.shape[0], cut), lambda k: (0, k)) for w in weights],
        out_specs=pl.BlockSpec((mine, cut), lambda k: (0, k)),
        name="term_%d" % at,
    )(keep, got, wq, wq2, *weights)


def per_device(
    norm_out, out_grad, attn_out, log_norm, query_weight, key_weight, value_weight, span_order
):
    shards = lax.axis_size("ctx")
    heads = lax.axis_size("head")
    odd = lax.axis_index("ctx") % 2 == 1
    rows = norm_out.shape[0]
    width = query_weight.shape[1]

    def flipped(array, axis, bit):
        return lax.ppermute(array, axis, [(i, i ^ bit) for i in range(lax.axis_size(axis))])

    def shifted(array, by):
        return lax.ppermute(array, "ctx", [(i, (i + by) % shards) for i in range(shards)])

    kw, vw = key_weight.T, value_weight.T
    kw2, vw2 = flipped(kw, "head", 1), flipped(vw, "head", 1)
    wq2 = flipped(query_weight, "head", 1)
    pack, far = project(
        norm_out, query_weight, kw, vw, kw2, vw2, out_grad, attn_out, log_norm
    )
    near = flipped(pack, "ctx", 1)
    far = lax.ppermute(
        far, "ctx", [(i, (i + (3 if i % 2 else -3)) % shards) for i in range(shards)]
    )
    own_kv, near_kv = pack[:rows, 2 * width :], near[:rows, 2 * width :]
    earlier = shifted(jnp.concatenate([own_kv, near_kv], axis=0), 2)
    later = shifted(jnp.concatenate([pack[:, : 2 * width], near[:, : 2 * width]], axis=0), -2)
    third = jnp.where(odd, near_kv, far[:rows, :width])
    kva = jnp.concatenate([own_kv, earlier, third], axis=0)
    kvx = flipped(kva, "head", 2)
    kw3, vw3 = flipped(kw, "head", 2), flipped(vw, "head", 2)
    kw4, vw4 = flipped(kw3, "head", 1), flipped(vw3, "head", 1)
    weights = (kw, vw, kw2, vw2, kw3, vw3, kw4, vw4)
    grads = attention(span_order, pack, near, far, later, kva, kvx)
    if heads != GROUP:
        full = nt(grads[:, :width], query_weight)
        full = full + nn(grads[:, width:], jnp.concatenate(weights, axis=0))
        return lax.psum_scatter(full.astype(BF16), "head", scatter_dimension=0, tiled=True)
    mine = rows // heads
    send, keep = split_rows(grads, mine)
    got = flipped(send, "head", 1)
    away = term(0, mine, keep, got, query_weight, wq2, weights, BF16)
    arrived = flipped(away, "head", 2)
    stay = term(1, mine, keep, got, query_weight, wq2, weights, F32)
    return (stay + arrived.astype(F32)).astype(BF16)


def solution(mesh):
    in_specs = (
        P("ctx", None),
        P("ctx", "head"),
        P("ctx", "head"),
        P("head", "ctx"),
        P(None, "head"),
        P(None, "head"),
        P(None, "head"),
        P(),
    )
    out_specs = P(("ctx", "head"), None)
    return jax.shard_map(
        per_device, mesh=mesh, in_specs=in_specs, out_specs=out_specs, check_vma=False
    )
```

```python
import functools

import jax
import jax.numpy as jnp
from jax import lax
from jax.experimental import pallas as pl
from jax.experimental.pallas import tpu as pltpu
from jax.sharding import PartitionSpec as P


GROUP = 4
EXTRA = 8
CUTS = 4
GRANT = 16 * 2**20
F32 = jnp.float32
BF16 = jnp.bfloat16


def nn(left, right):
    return jnp.dot(left, right, preferred_element_type=F32)


def nt(left, right):
    return lax.dot_general(left, right, (((1,), (1,)), ((), ())), preferred_element_type=F32)


def tn(left, right):
    return lax.dot_general(left, right, (((0,), (0,)), ((), ())), preferred_element_type=F32)


def three_pieces(row):
    high = row.astype(BF16).astype(F32)
    rest = row - high
    middle = rest.astype(BF16).astype(F32)
    return high, middle, rest - middle


def first_kernel(
    norm_hbm, wq_hbm, kw_hbm, vw_hbm, grad_hbm, attn_hbm, lse_hbm,
    side_ref, norm_ref, wkv_ref, wq_ref, grad_ref, attn_ref, lse_ref, sems,
):
    rows, depth = norm_ref.shape
    width = wq_ref.shape[1]
    quarter = wkv_ref.shape[0] // 2
    cut = depth // CUTS

    def fetch(at, source, target):
        copy = pltpu.make_async_copy(source, target, sems.at[at])
        copy.start()
        return copy

    norms, weights = [], []
    for k in range(CUTS):
        part = slice(k * cut, (k + 1) * cut)
        norms.append(fetch(2 * k, norm_hbm.at[:, part], norm_ref.at[:, part]))
        weights.append(fetch(2 * k + 1, wq_hbm.at[part, :], wq_ref.at[part, :]))
    at = 2 * CUTS
    others = [
        fetch(at, grad_hbm, grad_ref),
        fetch(at + 1, attn_hbm, attn_ref),
        fetch(at + 2, lse_hbm, lse_ref),
        fetch(at + 3, kw_hbm, wkv_ref.at[0:quarter, :]),
        fetch(at + 4, vw_hbm, wkv_ref.at[quarter : 2 * quarter, :]),
    ]
    query = jnp.zeros((rows, width), F32)
    for k in range(CUTS):
        part = slice(k * cut, (k + 1) * cut)
        norms[k].wait()
        weights[k].wait()
        query = query + nn(norm_ref[:, part], wq_ref[part, :])
    for copy in others:
        copy.wait()
    grad = grad_ref[...]
    prod = grad.astype(F32) * attn_ref[...].astype(F32)
    high = prod.astype(BF16)
    low = (prod - high.astype(F32)).astype(BF16)
    ones = jnp.ones((8, width), BF16)
    delta = (nt(ones, high) + nt(ones, low))[0:1, :]
    index = lax.broadcasted_iota(jnp.int32, (EXTRA, rows), 0)
    extra = jnp.zeros((EXTRA, rows), F32)
    for at, piece in enumerate(three_pieces(lse_ref[...]) + three_pieces(delta)):
        extra = jnp.where(index == at, piece, extra)
    side_ref[0:rows, 0:width] = query.astype(BF16)
    side_ref[0:rows, width:] = grad
    side_ref[rows:, :] = jnp.zeros((EXTRA, 2 * width), BF16)
    side_ref[rows:, 0:rows] = extra.astype(BF16)


def second_kernel(norm_ref, wkv_ref, kw2_ref, vw2_ref, side_ref, keyval_ref, far_ref):
    rows, width = keyval_ref.shape
    odd = lax.axis_index("ctx") % 2 == 1
    pair = jnp.concatenate([wkv_ref[...], kw2_ref[...], vw2_ref[...]], axis=0)
    keyval = nt(norm_ref[...], pair).astype(BF16)
    keyval_ref[...] = keyval

    @pl.when(odd)
    def _():
        far_ref[0:rows, 0:width] = keyval
        far_ref[0:rows, width:] = keyval
        far_ref[rows:, :] = jnp.zeros((EXTRA, 2 * width), BF16)

    @pl.when(jnp.logical_not(odd))
    def _():
        far_ref[...] = side_ref[...]


def stack_kernel(*refs):
    out_ref = refs[-1]
    at = 0
    for ref in refs[:-1]:
        out_ref[at : at + ref.shape[0], :] = ref[...]
        at += ref.shape[0]


def third_kernel(own_ref, near_ref, far_ref, out_ref):
    rows, width = own_ref.shape
    odd = lax.axis_index("ctx") % 2 == 1
    out_ref[0:rows, :] = own_ref[...]

    @pl.when(odd)
    def _():
        out_ref[rows:, :] = near_ref[...]

    @pl.when(jnp.logical_not(odd))
    def _():
        out_ref[rows:, :] = far_ref[0:rows, 0:width]


def local(body, outs, args, spaces=None, scratch=()):
    spaces = spaces or [pltpu.VMEM] * len(args)
    vmem = pl.BlockSpec(memory_space=pltpu.VMEM)
    many = isinstance(outs, tuple)
    shapes = tuple(jax.ShapeDtypeStruct(*o) for o in outs) if many else jax.ShapeDtypeStruct(*outs[0])
    args = [
        pltpu.with_memory_space_constraint(a, pltpu.HBM) if space is pltpu.HBM else a
        for a, space in zip(args, spaces)
    ]
    return pl.pallas_call(
        body,
        out_shape=shapes,
        in_specs=[pl.BlockSpec(memory_space=space) for space in spaces],
        out_specs=tuple(vmem for _ in outs) if many else vmem,
        scratch_shapes=list(scratch),
        compiler_params=pltpu.CompilerParams(vmem_limit_bytes=GRANT),
    )(*args)


def attention_kernel(
    span_ref, side_ref, near_ref, far_ref, later_ref, kva1_ref, kvx1_ref, kva2_ref, kvx2_ref, out_ref
):
    padded = side_ref.shape[0]
    rows = padded - EXTRA
    half = rows // 2
    width = kva1_ref.shape[1]
    quarter = width // GROUP
    scale = width ** (-0.5)
    shards = lax.axis_size("ctx")
    here = lax.axis_index("ctx")
    odd = here % 2 == 1
    member = lax.axis_index("head") % GROUP

    source = lax.broadcasted_iota(jnp.int32, (width, 2 * width), 0)
    target = lax.broadcasted_iota(jnp.int32, (width, 2 * width), 1)
    place = ((source // quarter) ^ member) * (2 * quarter) + source % quarter
    put_key = jnp.where(target == place, F32(1.0), F32(0.0)).astype(BF16)
    put_value = jnp.where(target == place + quarter, F32(1.0), F32(0.0)).astype(BF16)

    def positions(shard, axis):
        shape = (rows, 1) if axis == 0 else (1, rows)
        index = lax.broadcasted_iota(jnp.int32, shape, axis)
        first = span_ref[2 * shard]
        second = span_ref[2 * shard + 1]
        return jnp.where(index < half, first * half + index, (second - 1) * half + index)

    def queries(block, shard):
        spread = nn(block[0:rows, 0:width], put_key).astype(BF16)
        grad = nn(block[0:rows, width : 2 * width], put_value).astype(BF16)
        tail = block[rows : rows + 8, :].astype(F32)
        lse = tail[0:1, 0:rows] + tail[1:2, 0:rows] + tail[2:3, 0:rows]
        delta = tail[3:4, 0:rows] + tail[4:5, 0:rows] + tail[5:6, 0:rows]
        return spread, grad, lse, delta, positions(shard, 1)

    def keys(kva_ref, kvx_ref, at, shard):
        part = slice(at * rows, (at + 1) * rows)
        return jnp.concatenate([kva_ref[part, :], kvx_ref[part, :]], axis=1), positions(shard, 0)

    def block(query, key):
        spread, grad, lse, delta, query_pos = query
        keyval, key_pos = key
        scores = nt(keyval, spread) * scale
        prob = jnp.where(key_pos <= query_pos, jnp.exp(scores - lse), F32(0.0))
        dscore = prob * (nt(keyval, grad) - delta)
        return prob.astype(BF16), dscore.astype(BF16)

    def ring(shard):
        return (shard + 2 * shards) % shards

    before = ring(here - 2)
    after = ring(here + 2)
    flip = 1 - 2 * (here % 2)
    own_query = queries(side_ref[...], here)
    own_key = keys(kva1_ref, kvx1_ref, 0, here)

    prob, dscore = block(own_query, own_key)
    dquery = tn(dscore, own_key[0])
    dkey = nn(dscore, own_query[0])
    dvalue = nn(prob, own_query[1])
    for kva_ref, kvx_ref, at, shard in (
        (kva1_ref, kvx1_ref, 1, ring(jnp.where(odd, here - 1, here - 3))),
        (kva2_ref, kvx2_ref, 0, before),
        (kva2_ref, kvx2_ref, 1, ring(before + flip)),
    ):
        key = keys(kva_ref, kvx_ref, at, shard)
        _, dscore = block(own_query, key)
        dquery += tn(dscore, key[0])
    third = jnp.where(odd, far_ref[...], near_ref[...])
    for packed, shard in (
        (later_ref[0:padded, :], after),
        (later_ref[padded:, :], ring(after + flip)),
        (third, ring(jnp.where(odd, here + 3, here + 1))),
    ):
        query = queries(packed, shard)
        prob, dscore = block(query, own_key)
        dkey += nn(dscore, query[0])
        dvalue += nn(prob, query[1])
    dquery_b = (dquery * scale).astype(BF16)
    out_ref[:, 0:width] = nt(dquery_b, put_key).astype(BF16)
    out_ref[:, width:] = (dkey * scale + dvalue).astype(BF16)


def split_kernel(mine, grads_ref, send_ref, keep_ref):
    rows, columns = grads_ref.shape
    width = columns // 3
    padded = send_ref.shape[0] // 2
    member = lax.axis_index("head")
    grads = grads_ref[...]
    slot = lax.broadcasted_iota(jnp.int32, (padded, rows), 0)
    token = lax.broadcasted_iota(jnp.int32, (padded, rows), 1)

    def rows_of(owner):
        chosen = jnp.where((token == owner * mine + slot) & (slot < mine), F32(1.0), F32(0.0))
        return nn(chosen.astype(BF16), grads)

    for at, (other, kept) in enumerate(((3, 2), (1, 0))):
        part = slice(at * padded, (at + 1) * padded)
        keep_ref[part, :] = rows_of(member ^ kept).astype(BF16)
        sent = rows_of(member ^ other)
        send_ref[part, 0:width] = sent[:, 0:width].astype(BF16)
        for step in (1, 2):
            lanes = slice(step * width, (step + 1) * width)
            send_ref[part, lanes] = pltpu.roll(sent[:, lanes], width // 2, 1).astype(BF16)


def term_kernel(at, keep_ref, got_ref, wq_ref, wq2_ref, *refs):
    weights, out_ref = refs[:-1], refs[-1]
    mine, depth = out_ref.shape
    width = wq_ref.shape[1]
    padded = keep_ref.shape[0] // 2
    part = slice(at * padded, (at + 1) * padded)
    keep = keep_ref[part, :]
    got = got_ref[part, :]
    both = (keep[:, width:].astype(F32) + got[:, width:].astype(F32)).astype(BF16)
    cut = depth // CUTS
    for k in range(CUTS):
        cols = slice(k * cut, (k + 1) * cut)
        total = nt(keep[:, 0:width], wq_ref[cols, :]) + nt(got[:, 0:width], wq2_ref[cols, :])
        stacked = jnp.concatenate([w[:, cols] for w in weights], axis=0)
        total = total + nn(both, stacked)
        out_ref[:, cols] = total[0:mine, :].astype(out_ref.dtype)


def per_device(
    norm_out, out_grad, attn_out, log_norm, query_weight, key_weight, value_weight, span_order
):
    shards = lax.axis_size("ctx")
    heads = lax.axis_size("head")
    rows = norm_out.shape[0]
    width = query_weight.shape[1]

    def sent(array, axis, to):
        return lax.ppermute(array, axis, [(i, to(i)) for i in range(lax.axis_size(axis))])

    def flipped(array, axis, bit):
        return sent(array, axis, lambda i: i ^ bit)

    def shifted(array, by):
        return sent(array, "ctx", lambda i: (i + by) % shards)

    kw, vw = key_weight.T, value_weight.T
    quarter, depth = kw.shape
    kw2, vw2 = flipped(kw, "head", 1), flipped(vw, "head", 1)
    wq2 = flipped(query_weight, "head", 1)
    tall = rows + EXTRA
    side, norm, wkv = local(
        first_kernel,
        (((tall, 2 * width), BF16), ((rows, depth), BF16), ((2 * quarter, depth), BF16)),
        (norm_out, query_weight, kw, vw, out_grad, attn_out, log_norm),
        [pltpu.HBM] * 7,
        [
            pltpu.VMEM((depth, width), BF16),
            pltpu.VMEM((rows, width), BF16),
            pltpu.VMEM((rows, width), BF16),
            pltpu.VMEM((1, rows), F32),
            pltpu.SemaphoreType.DMA((2 * CUTS + 5,)),
        ],
    )
    wkv3 = flipped(wkv, "head", 2)
    keyval, far = local(
        second_kernel,
        (((rows, width), BF16), ((tall, 2 * width), BF16)),
        (norm, wkv, kw2, vw2, side),
    )
    near_kv = flipped(keyval, "ctx", 1)
    near = flipped(side, "ctx", 1)
    far = sent(far, "ctx", lambda i: (i + (3 if i % 2 else -3)) % shards)
    pair_kv = local(stack_kernel, [((2 * rows, width), BF16)], (keyval, near_kv))
    kva2 = shifted(pair_kv, 2)
    pair_side = local(stack_kernel, [((2 * tall, 2 * width), BF16)], (side, near))
    later = shifted(pair_side, -2)
    kva1 = local(third_kernel, [((2 * rows, width), BF16)], (keyval, near_kv, far))
    kvx1 = flipped(kva1, "head", 2)
    kvx2 = flipped(kva2, "head", 2)
    wkv4 = flipped(wkv3, "head", 1)
    weights = (wkv, kw2, vw2, wkv3, wkv4)
    grads = local(
        attention_kernel,
        [((rows, 3 * width), BF16)],
        (span_order, side, near, far, later, kva1, kvx1, kva2, kvx2),
        [pltpu.SMEM] + [pltpu.VMEM] * 8,
    )
    if heads != GROUP:
        full = nt(grads[:, :width], query_weight)
        full = full + nn(grads[:, width:], jnp.concatenate(weights, axis=0))
        return lax.psum_scatter(full.astype(BF16), "head", scatter_dimension=0, tiled=True)
    mine = rows // heads
    padded = -(-mine // 8) * 8
    block = ((2 * padded, 3 * width), BF16)
    send, keep = local(functools.partial(split_kernel, mine), (block, block), (grads,))
    got = flipped(send, "head", 1)
    operands = (keep, got, query_weight, wq2) + weights
    away = local(functools.partial(term_kernel, 0), [((mine, depth), BF16)], operands)
    arrived = flipped(away, "head", 2)
    stay = local(functools.partial(term_kernel, 1), [((mine, depth), F32)], operands)
    return (stay + arrived.astype(F32)).astype(BF16)


def solution(mesh):
    in_specs = (
        P("ctx", None),
        P("ctx", "head"),
        P("ctx", "head"),
        P("head", "ctx"),
        P(None, "head"),
        P(None, "head"),
        P(None, "head"),
        P(),
    )
    out_specs = P(("ctx", "head"), None)

    return jax.shard_map(
        per_device, mesh=mesh, in_specs=in_specs, out_specs=out_specs, check_vma=False
    )
```

```python
import functools

import jax
import jax.numpy as jnp
from jax import lax
from jax.experimental import pallas as pl
from jax.experimental.pallas import tpu as pltpu
from jax.sharding import PartitionSpec as P


GROUP = 4
EXTRA = 8
CUTS = 4
GRANT = 16 * 2**20
F32 = jnp.float32
BF16 = jnp.bfloat16


def nn(left, right):
    return jnp.dot(left, right, preferred_element_type=F32)


def nt(left, right):
    return lax.dot_general(left, right, (((1,), (1,)), ((), ())), preferred_element_type=F32)


def tn(left, right):
    return lax.dot_general(left, right, (((0,), (0,)), ((), ())), preferred_element_type=F32)


def three_pieces(row):
    high = row.astype(BF16).astype(F32)
    rest = row - high
    middle = rest.astype(BF16).astype(F32)
    return high, middle, rest - middle


def first_kernel(
    norm_hbm, wq_hbm, kw_hbm, vw_hbm, grad_hbm, attn_hbm, lse_hbm,
    side_ref, norm_ref, wkv_ref, wq_ref, grad_ref, attn_ref, lse_ref, sems,
):
    rows, depth = norm_ref.shape
    width = wq_ref.shape[1]
    quarter = wkv_ref.shape[0] // 2
    cut = depth // CUTS

    def fetch(at, source, target):
        copy = pltpu.make_async_copy(source, target, sems.at[at])
        copy.start()
        return copy

    norms, weights = [], []
    for k in range(CUTS):
        part = slice(k * cut, (k + 1) * cut)
        norms.append(fetch(2 * k, norm_hbm.at[:, part], norm_ref.at[:, part]))
        weights.append(fetch(2 * k + 1, wq_hbm.at[part, :], wq_ref.at[part, :]))
    at = 2 * CUTS
    others = [
        fetch(at, grad_hbm, grad_ref),
        fetch(at + 1, attn_hbm, attn_ref),
        fetch(at + 2, lse_hbm, lse_ref),
        fetch(at + 3, kw_hbm, wkv_ref.at[0:quarter, :]),
        fetch(at + 4, vw_hbm, wkv_ref.at[quarter : 2 * quarter, :]),
    ]
    query = jnp.zeros((rows, width), F32)
    for k in range(CUTS):
        part = slice(k * cut, (k + 1) * cut)
        norms[k].wait()
        weights[k].wait()
        query = query + nn(norm_ref[:, part], wq_ref[part, :])
    for copy in others:
        copy.wait()
    grad = grad_ref[...]
    prod = grad.astype(F32) * attn_ref[...].astype(F32)
    high = prod.astype(BF16)
    low = (prod - high.astype(F32)).astype(BF16)
    ones = jnp.ones((8, width), BF16)
    delta = (nt(ones, high) + nt(ones, low))[0:1, :]
    index = lax.broadcasted_iota(jnp.int32, (EXTRA, rows), 0)
    extra = jnp.zeros((EXTRA, rows), F32)
    for at, piece in enumerate(three_pieces(lse_ref[...]) + three_pieces(delta)):
        extra = jnp.where(index == at, piece, extra)
    side_ref[0:rows, 0:width] = query.astype(BF16)
    side_ref[0:rows, width:] = grad
    side_ref[rows:, :] = jnp.zeros((EXTRA, 2 * width), BF16)
    side_ref[rows:, 0:rows] = extra.astype(BF16)


def second_kernel(norm_ref, wkv_ref, kw2_ref, vw2_ref, side_ref, keyval_ref, far_ref):
    rows, width = keyval_ref.shape
    odd = lax.axis_index("ctx") % 2 == 1
    pair = jnp.concatenate([wkv_ref[...], kw2_ref[...], vw2_ref[...]], axis=0)
    keyval = nt(norm_ref[...], pair).astype(BF16)
    keyval_ref[...] = keyval

    @pl.when(odd)
    def _():
        far_ref[0:rows, 0:width] = keyval
        far_ref[0:rows, width:] = keyval
        far_ref[rows:, :] = jnp.zeros((EXTRA, 2 * width), BF16)

    @pl.when(jnp.logical_not(odd))
    def _():
        far_ref[...] = side_ref[...]


def stack_kernel(*refs):
    out_ref = refs[-1]
    at = 0
    for ref in refs[:-1]:
        out_ref[at : at + ref.shape[0], :] = ref[...]
        at += ref.shape[0]


def third_kernel(own_ref, near_ref, far_ref, out_ref):
    rows, width = own_ref.shape
    odd = lax.axis_index("ctx") % 2 == 1
    out_ref[0:rows, :] = own_ref[...]

    @pl.when(odd)
    def _():
        out_ref[rows:, :] = near_ref[...]

    @pl.when(jnp.logical_not(odd))
    def _():
        out_ref[rows:, :] = far_ref[0:rows, 0:width]


def local(body, outs, args, spaces=None, scratch=()):
    spaces = spaces or [pltpu.VMEM] * len(args)
    vmem = pl.BlockSpec(memory_space=pltpu.VMEM)
    many = isinstance(outs, tuple)
    shapes = tuple(jax.ShapeDtypeStruct(*o) for o in outs) if many else jax.ShapeDtypeStruct(*outs[0])
    args = [
        pltpu.with_memory_space_constraint(a, pltpu.HBM) if space is pltpu.HBM else a
        for a, space in zip(args, spaces)
    ]
    return pl.pallas_call(
        body,
        out_shape=shapes,
        in_specs=[pl.BlockSpec(memory_space=space) for space in spaces],
        out_specs=tuple(vmem for _ in outs) if many else vmem,
        scratch_shapes=list(scratch),
        compiler_params=pltpu.CompilerParams(vmem_limit_bytes=GRANT),
    )(*args)


def ring(shard):
    shards = lax.axis_size("ctx")
    return (shard + 2 * shards) % shards


def placing(width):
    quarter = width // GROUP
    member = lax.axis_index("head") % GROUP
    source = lax.broadcasted_iota(jnp.int32, (width, 2 * width), 0)
    target = lax.broadcasted_iota(jnp.int32, (width, 2 * width), 1)
    place = ((source // quarter) ^ member) * (2 * quarter) + source % quarter
    put_key = jnp.where(target == place, F32(1.0), F32(0.0)).astype(BF16)
    put_value = jnp.where(target == place + quarter, F32(1.0), F32(0.0)).astype(BF16)
    return put_key, put_value


def positions(span_ref, shard, rows, axis):
    half = rows // 2
    shape = (rows, 1) if axis == 0 else (1, rows)
    index = lax.broadcasted_iota(jnp.int32, shape, axis)
    first = span_ref[2 * shard]
    second = span_ref[2 * shard + 1]
    return jnp.where(index < half, first * half + index, (second - 1) * half + index)


def pieces_sum(tail, at, rows):
    row = tail[at : at + 1, :] + tail[at + 1 : at + 2, :] + tail[at + 2 : at + 3, :]
    return row[:, 0:rows]


def chosen_rows(mine, rows, padded):
    member = lax.axis_index("head")
    slot = lax.broadcasted_iota(jnp.int32, (4 * padded, rows), 0)
    token = lax.broadcasted_iota(jnp.int32, (4 * padded, rows), 1)
    inside = slot % padded
    owner = jnp.where(slot < padded, member ^ 3, member ^ 1)
    owner = jnp.where(slot >= 2 * padded, member ^ 2, owner)
    owner = jnp.where(slot >= 3 * padded, member, owner)
    chosen = jnp.where((token == owner * mine + inside) & (inside < mine), F32(1.0), F32(0.0))
    return chosen.astype(BF16)


def attention_kernel(
    mine, span_ref, side_ref, near_ref, far_ref, later_ref, kva1_ref, kvx1_ref, kva2_ref, kvx2_ref,
    *outs,
):
    padded = side_ref.shape[0]
    rows = padded - EXTRA
    width = kva1_ref.shape[1]
    scale = width ** (-0.5)
    log2e = 1.4426950408889634
    here = lax.axis_index("ctx")
    odd = here % 2 == 1
    flip = 1 - 2 * (here % 2)
    put_key, put_value = placing(width)
    before, after = ring(here - 2), ring(here + 2)
    key_shards = (here, ring(jnp.where(odd, here - 1, here - 3)), before, ring(before + flip))
    query_shards = (here, ring(jnp.where(odd, here + 3, here + 1)), after, ring(after + flip))

    keyval = jnp.concatenate(
        [
            jnp.concatenate([kva1_ref[...], kvx1_ref[...]], axis=1),
            jnp.concatenate([kva2_ref[...], kvx2_ref[...]], axis=1),
        ],
        axis=0,
    )
    third = jnp.where(odd, far_ref[...], near_ref[...])
    blocks = (side_ref[...], third, later_ref[0:padded, :], later_ref[padded:, :])
    spread = nn(jnp.concatenate([b[0:rows, 0:width] for b in blocks], axis=0), put_key)
    grad = nn(jnp.concatenate([b[0:rows, width:] for b in blocks], axis=0), put_value)
    spread, grad = spread.astype(BF16), grad.astype(BF16)
    tails = [b[rows:, :].astype(F32) for b in blocks]
    lse_row = jnp.concatenate([pieces_sum(t, 0, rows) for t in tails], axis=1)
    delta_row = jnp.concatenate([pieces_sum(t, 3, rows) for t in tails], axis=1)

    own_tail = blocks[0][rows:, 0:rows]
    index = lax.broadcasted_iota(jnp.int32, (EXTRA, 128), 0)
    first_three = jnp.where(index < 3, F32(1.0), F32(0.0)).astype(BF16)
    next_three = jnp.where((index >= 3) & (index < 6), F32(1.0), F32(0.0)).astype(BF16)
    lse_col = tn(own_tail, first_three)[:, 0:1]
    delta_col = tn(own_tail, next_three)[:, 0:1]

    query_pos = positions(span_ref, here, rows, 0)
    key_pos = jnp.concatenate([positions(span_ref, s, rows, 1) for s in key_shards], axis=1)
    scores = nt(spread[0:rows], keyval) * (scale * log2e)
    prob = jnp.where(key_pos <= query_pos, jnp.exp2(scores - lse_col * log2e), F32(0.0))
    dscore = prob * (nt(grad[0:rows], keyval) - delta_col)
    keyabs = nt(keyval, put_key).astype(BF16)
    dquery = (nn(dscore.astype(BF16), keyabs) * scale).astype(BF16)

    own = keyval[0:rows]
    key_pos = positions(span_ref, here, rows, 0)
    query_pos = jnp.concatenate([positions(span_ref, s, rows, 1) for s in query_shards], axis=1)
    scores = nt(own, spread) * (scale * log2e)
    prob = jnp.where(key_pos <= query_pos, jnp.exp2(scores - lse_row * log2e), F32(0.0))
    dscore = prob * (nt(own, grad) - delta_row)
    dkv = nn(dscore.astype(BF16), spread) * scale + nn(prob.astype(BF16), grad)
    dkv = dkv.astype(BF16)
    if mine is None:
        outs[0][:, 0:width] = dquery
        outs[0][:, width:] = dkv
        return
    send_ref, keep_ref = outs
    half = send_ref.shape[0]
    chosen = chosen_rows(mine, rows, half // 2)
    picked = nn(chosen, dquery).astype(BF16)
    send_ref[:, 0:width] = picked[0:half]
    keep_ref[:, 0:width] = picked[half:]
    picked = nn(chosen, dkv)
    keep_ref[:, width:] = picked[half:].astype(BF16)
    for step in (0, 1):
        lanes = slice(step * width, (step + 1) * width)
        rolled = pltpu.roll(picked[0:half, lanes], width // 2, 1).astype(BF16)
        send_ref[:, (step + 1) * width : (step + 2) * width] = rolled


def term_kernel(at, cuts, keep_ref, got_ref, wq_ref, wq2_ref, *refs):
    weights, outs = refs[: -len(cuts)], refs[-len(cuts) :]
    width = wq_ref.shape[1]
    padded = keep_ref.shape[0] // 2
    part = slice(at * padded, (at + 1) * padded)
    keep, got = keep_ref[part, 0:width], got_ref[part, 0:width]
    both = keep_ref[part, width:].astype(F32) + got_ref[part, width:].astype(F32)
    both = both.astype(BF16)
    for (start, stop), out_ref in zip(cuts, outs):
        mine = out_ref.shape[0]
        cut = (stop - start) // 2
        for k in range(2):
            cols = slice(start + k * cut, start + (k + 1) * cut)
            total = nt(keep, wq_ref[cols, :]) + nt(got, wq2_ref[cols, :])
            stacked = jnp.concatenate([w[:, cols] for w in weights], axis=0)
            total = total + nn(both, stacked)
            out_ref[:, k * cut : (k + 1) * cut] = total[0:mine, :].astype(out_ref.dtype)


def add_kernel(*refs):
    count = (len(refs) - 1) // 2
    stays, arrivals, out_ref = refs[:count], refs[count:-1], refs[-1]
    at = 0
    for stay, arrived in zip(stays, arrivals):
        cols = slice(at, at + stay.shape[1])
        out_ref[:, cols] = (stay[...] + arrived[...].astype(F32)).astype(BF16)
        at += stay.shape[1]


def per_device(
    norm_out, out_grad, attn_out, log_norm, query_weight, key_weight, value_weight, span_order
):
    shards = lax.axis_size("ctx")
    heads = lax.axis_size("head")
    rows = norm_out.shape[0]
    width = query_weight.shape[1]

    def sent(array, axis, to):
        return lax.ppermute(array, axis, [(i, to(i)) for i in range(lax.axis_size(axis))])

    def flipped(array, axis, bit):
        return sent(array, axis, lambda i: i ^ bit)

    def shifted(array, by):
        return sent(array, "ctx", lambda i: (i + by) % shards)

    kw, vw = key_weight.T, value_weight.T
    quarter, depth = kw.shape
    kw2, vw2 = flipped(kw, "head", 1), flipped(vw, "head", 1)
    wq2 = flipped(query_weight, "head", 1)
    tall = rows + EXTRA
    side, norm, wkv = local(
        first_kernel,
        (((tall, 2 * width), BF16), ((rows, depth), BF16), ((2 * quarter, depth), BF16)),
        (norm_out, query_weight, kw, vw, out_grad, attn_out, log_norm),
        [pltpu.HBM] * 7,
        [
            pltpu.VMEM((depth, width), BF16),
            pltpu.VMEM((rows, width), BF16),
            pltpu.VMEM((rows, width), BF16),
            pltpu.VMEM((1, rows), F32),
            pltpu.SemaphoreType.DMA((2 * CUTS + 5,)),
        ],
    )
    wkv3 = flipped(wkv, "head", 2)
    keyval, far = local(
        second_kernel,
        (((rows, width), BF16), ((tall, 2 * width), BF16)),
        (norm, wkv, kw2, vw2, side),
    )
    near_kv = flipped(keyval, "ctx", 1)
    near = flipped(side, "ctx", 1)
    far = sent(far, "ctx", lambda i: (i + (3 if i % 2 else -3)) % shards)
    pair_kv = local(stack_kernel, [((2 * rows, width), BF16)], (keyval, near_kv))
    kva2 = shifted(pair_kv, 2)
    pair_side = local(stack_kernel, [((2 * tall, 2 * width), BF16)], (side, near))
    later = shifted(pair_side, -2)
    kva1 = local(third_kernel, [((2 * rows, width), BF16)], (keyval, near_kv, far))
    kvx1 = flipped(kva1, "head", 2)
    kvx2 = flipped(kva2, "head", 2)
    wkv4 = flipped(wkv3, "head", 1)
    weights = (wkv, kw2, vw2, wkv3, wkv4)
    fast = heads == GROUP
    mine = rows // heads if fast else None
    tall = 2 * (-(-rows // heads // 8) * 8)
    outs = (((tall, 3 * width), BF16),) * 2 if fast else [((rows, 3 * width), BF16)]
    grads = local(
        functools.partial(attention_kernel, mine),
        outs,
        (span_order, side, near, far, later, kva1, kvx1, kva2, kvx2),
        [pltpu.SMEM] + [pltpu.VMEM] * 8,
    )
    if not fast:
        full = nt(grads[:, :width], query_weight)
        full = full + nn(grads[:, width:], jnp.concatenate(weights, axis=0))
        return lax.psum_scatter(full.astype(BF16), "head", scatter_dimension=0, tiled=True)
    send, keep = grads
    got = flipped(send, "head", 1)
    operands = (keep, got, query_weight, wq2) + weights
    half = depth // 2
    halves = ((0, half), (half, depth))
    arrived = []
    for cut in halves:
        away = local(functools.partial(term_kernel, 0, (cut,)), [((mine, half), BF16)], operands)
        arrived.append(flipped(away, "head", 2))
    stays = local(
        functools.partial(term_kernel, 1, halves),
        (((mine, half), F32), ((mine, half), F32)),
        operands,
    )
    return local(add_kernel, [((mine, depth), BF16)], tuple(stays) + tuple(arrived))


def solution(mesh):
    in_specs = (
        P("ctx", None),
        P("ctx", "head"),
        P("ctx", "head"),
        P("head", "ctx"),
        P(None, "head"),
        P(None, "head"),
        P(None, "head"),
        P(),
    )
    out_specs = P(("ctx", "head"), None)

    return jax.shard_map(
        per_device, mesh=mesh, in_specs=in_specs, out_specs=out_specs, check_vma=False
    )
```

```python
import functools

import jax
import jax.numpy as jnp
from jax import lax
from jax.experimental import pallas as pl
from jax.experimental.pallas import tpu as pltpu
from jax.sharding import PartitionSpec as P


GROUP = 4
EXTRA = 8
GRANT = 16 * 2**20
F32 = jnp.float32
BF16 = jnp.bfloat16


def nn(left, right):
    return jnp.dot(left, right, preferred_element_type=F32)


def nt(left, right):
    return lax.dot_general(left, right, (((1,), (1,)), ((), ())), preferred_element_type=F32)


def tn(left, right):
    return lax.dot_general(left, right, (((0,), (0,)), ((), ())), preferred_element_type=F32)


def three_pieces(row):
    high = row.astype(BF16).astype(F32)
    rest = row - high
    middle = rest.astype(BF16).astype(F32)
    return high, middle, rest - middle


def load_kernel(*refs):
    sources, (norm_ref, wkv_ref, grad_ref, attn_ref, lse_ref, sems) = refs[:6], refs[6:]
    quarter = wkv_ref.shape[0] // 2
    half = norm_ref.shape[1] // 2
    norm, kw, vw, grad, attn, lse = sources
    pairs = (
        (norm.at[:, 0:half], norm_ref.at[:, 0:half]),
        (norm.at[:, half:], norm_ref.at[:, half:]),
        (kw, wkv_ref.at[0:quarter, :]),
        (vw, wkv_ref.at[quarter:, :]),
        (grad, grad_ref),
        (attn, attn_ref),
        (lse, lse_ref),
    )
    copies = [pltpu.make_async_copy(a, b, sems.at[k]) for k, (a, b) in enumerate(pairs)]
    for copy in copies:
        copy.start()
    for copy in copies:
        copy.wait()


def keyval_kernel(norm_ref, wkv_ref, kw2_ref, vw2_ref, keyval_ref):
    width = keyval_ref.shape[1]
    quarter = kw2_ref.shape[0]
    upper = lax.axis_index("head") // 2 % 2 == 1
    own = wkv_ref[...]
    pair = jnp.concatenate([own[0:quarter], kw2_ref[...], own[quarter:], vw2_ref[...]], axis=0)
    keyval = nt(norm_ref[...], pair)
    keyval_ref[...] = jnp.where(upper, pltpu.roll(keyval, width // 2, 1), keyval).astype(BF16)


def query_kernel(norm_ref, wq_ref, grad_ref, attn_ref, lse_ref, keyval_ref, side_ref, far_ref):
    rows, width = grad_ref.shape
    odd = lax.axis_index("ctx") % 2 == 1
    core = lax.axis_index("head") % 2
    query = nn(norm_ref[...], wq_ref[...]).astype(BF16)
    grad = grad_ref[...]
    prod = grad.astype(F32) * attn_ref[...].astype(F32)
    high = prod.astype(BF16)
    low = (prod - high.astype(F32)).astype(BF16)
    ones = jnp.ones((8, width), BF16)
    delta = (nt(ones, high) + nt(ones, low))[0:1, :]
    index = lax.broadcasted_iota(jnp.int32, (EXTRA, rows), 0)
    extra = jnp.zeros((EXTRA, rows), F32)
    for at, piece in enumerate(three_pieces(lse_ref[...]) + three_pieces(delta)):
        extra = jnp.where(index == at, piece, extra)
    side_ref[0:rows, width:] = reordered(grad, core ^ 2)
    side_ref[rows:, :] = jnp.zeros((EXTRA, 2 * width), BF16)
    side_ref[rows:, 0:rows] = extra.astype(BF16)
    side_ref[0:rows, 0:width] = jnp.where(
        core == 1, swapped_quarters(query.astype(F32)), query.astype(F32)
    ).astype(BF16)

    @pl.when(odd)
    def _():
        far_ref[0:rows, 0:width] = keyval_ref[...]
        far_ref[0:rows, width:] = keyval_ref[...]
        far_ref[rows:, :] = jnp.zeros((EXTRA, 2 * width), BF16)

    @pl.when(jnp.logical_not(odd))
    def _():
        far_ref[...] = side_ref[...]


def stack_kernel(*refs):
    out_ref = refs[-1]
    at = 0
    for ref in refs[:-1]:
        out_ref[at : at + ref.shape[0], :] = ref[...]
        at += ref.shape[0]


def third_kernel(own_ref, near_ref, far_ref, out_ref):
    rows, width = own_ref.shape
    odd = lax.axis_index("ctx") % 2 == 1
    out_ref[0:rows, :] = own_ref[...]

    @pl.when(odd)
    def _():
        out_ref[rows:, :] = near_ref[...]

    @pl.when(jnp.logical_not(odd))
    def _():
        out_ref[rows:, :] = far_ref[0:rows, 0:width]


def local(body, outs, args, spaces=None, scratch=()):
    spaces = spaces or [pltpu.VMEM] * len(args)
    vmem = pl.BlockSpec(memory_space=pltpu.VMEM)
    many = isinstance(outs, tuple)
    shapes = tuple(jax.ShapeDtypeStruct(*o) for o in outs) if many else jax.ShapeDtypeStruct(*outs[0])
    args = [
        pltpu.with_memory_space_constraint(a, pltpu.HBM) if space is pltpu.HBM else a
        for a, space in zip(args, spaces)
    ]
    return pl.pallas_call(
        body,
        out_shape=shapes,
        in_specs=[pl.BlockSpec(memory_space=space) for space in spaces],
        out_specs=tuple(vmem for _ in outs) if many else vmem,
        scratch_shapes=list(scratch),
        compiler_params=pltpu.CompilerParams(vmem_limit_bytes=GRANT),
    )(*args)


def ring(shard):
    shards = lax.axis_size("ctx")
    return (shard + 2 * shards) % shards


def reordered(array, flip):
    width = array.shape[1]
    quarter = width // GROUP
    source = lax.broadcasted_iota(jnp.int32, (width, width), 0)
    target = lax.broadcasted_iota(jnp.int32, (width, width), 1)
    moved = ((source // quarter) ^ flip) * quarter + source % quarter
    return nn(array, jnp.where(target == moved, F32(1.0), F32(0.0)).astype(BF16)).astype(BF16)


def swapped_quarters(array):
    width = array.shape[1]
    quarter = width // GROUP
    lane = lax.broadcasted_iota(jnp.int32, array.shape, 1)
    left = pltpu.roll(array, width - quarter, 1)
    right = pltpu.roll(array, quarter, 1)
    return jnp.where((lane // quarter) % 2 == 0, left, right)


def positions(span_ref, shard, rows, axis):
    half = rows // 2
    shape = (rows, 1) if axis == 0 else (1, rows)
    index = lax.broadcasted_iota(jnp.int32, shape, axis)
    first = span_ref[2 * shard]
    second = span_ref[2 * shard + 1]
    return jnp.where(index < half, first * half + index, (second - 1) * half + index)


def pieces_sum(tail, at, rows):
    row = tail[at : at + 1, :] + tail[at + 1 : at + 2, :] + tail[at + 2 : at + 3, :]
    return row[:, 0:rows]


def chosen_rows(mine, rows, padded):
    member = lax.axis_index("head")
    slot = lax.broadcasted_iota(jnp.int32, (4 * padded, rows), 0)
    token = lax.broadcasted_iota(jnp.int32, (4 * padded, rows), 1)
    inside = slot % padded
    owner = jnp.where(slot < padded, member ^ 3, member ^ 1)
    owner = jnp.where(slot >= 2 * padded, member ^ 2, owner)
    owner = jnp.where(slot >= 3 * padded, member, owner)
    chosen = jnp.where((token == owner * mine + inside) & (inside < mine), F32(1.0), F32(0.0))
    return chosen.astype(BF16)


def attention_kernel(
    mine, span_ref, side_ref, near_ref, far_ref, later_ref, kva1_ref, kvx1_ref, kva2_ref, kvx2_ref,
    *outs,
):
    padded = side_ref.shape[0]
    rows = padded - EXTRA
    width = kva1_ref.shape[1]
    scale = width ** (-0.5)
    log2e = 1.4426950408889634
    here = lax.axis_index("ctx")
    head = lax.axis_index("head")
    core, upper = head % 2, head // 2 % 2
    odd = here % 2 == 1
    flip = 1 - 2 * (here % 2)
    before, after = ring(here - 2), ring(here + 2)
    key_shards = (here, ring(jnp.where(odd, here - 1, here - 3)), before, ring(before + flip))
    query_shards = (here, ring(jnp.where(odd, here + 3, here + 1)), after, ring(after + flip))

    mixed = jnp.concatenate([kva1_ref[...], kva2_ref[...]], axis=0)
    other = jnp.concatenate([kvx1_ref[...], kvx2_ref[...]], axis=0)
    lane = lax.broadcasted_iota(jnp.int32, mixed.shape, 1)
    here_first = (lane // (width // 2)) == upper
    key = jnp.where(here_first, mixed, other)
    value = jnp.where(here_first, other, mixed)
    third = jnp.where(odd, far_ref[...], near_ref[...])
    blocks = (side_ref[...], third, later_ref[0:padded, :], later_ref[padded:, :])
    query = jnp.concatenate([b[0:rows, 0:width] for b in blocks], axis=0)
    grad = jnp.concatenate([b[0:rows, width:] for b in blocks], axis=0)
    tails = [b[rows:, :].astype(F32) for b in blocks]
    lse_row = jnp.concatenate([pieces_sum(t, 0, rows) for t in tails], axis=1)
    delta_row = jnp.concatenate([pieces_sum(t, 3, rows) for t in tails], axis=1)

    own_tail = blocks[0][rows:, 0:rows]
    index = lax.broadcasted_iota(jnp.int32, (EXTRA, 128), 0)
    first_three = jnp.where(index < 3, F32(1.0), F32(0.0)).astype(BF16)
    next_three = jnp.where((index >= 3) & (index < 6), F32(1.0), F32(0.0)).astype(BF16)
    lse_col = tn(own_tail, first_three)[:, 0:1]
    delta_col = tn(own_tail, next_three)[:, 0:1]

    query_pos = positions(span_ref, here, rows, 0)
    key_pos = jnp.concatenate([positions(span_ref, s, rows, 1) for s in key_shards], axis=1)
    scores = nt(query[0:rows], key) * (scale * log2e)
    prob = jnp.where(key_pos <= query_pos, jnp.exp2(scores - lse_col * log2e), F32(0.0))
    dscore = prob * (nt(grad[0:rows], value) - delta_col)
    dquery = (nn(dscore.astype(BF16), key) * scale).astype(BF16)

    key_pos = positions(span_ref, here, rows, 0)
    query_pos = jnp.concatenate([positions(span_ref, s, rows, 1) for s in query_shards], axis=1)
    scores = nt(key[0:rows], query) * (scale * log2e)
    prob = jnp.where(key_pos <= query_pos, jnp.exp2(scores - lse_row * log2e), F32(0.0))
    dscore = prob * (nt(value[0:rows], grad) - delta_row)
    dkey = (nn(dscore.astype(BF16), query) * scale).astype(BF16)
    dvalue = nn(prob.astype(BF16), grad).astype(BF16)

    def placed(array, step):
        if step == 0:
            return jnp.where(core == 1, swapped_quarters(array), array)
        return jnp.where(upper == 2 - step, pltpu.roll(array, width // 2, 1), array)

    results = (dquery, dkey, dvalue)
    if mine is None:
        for step, result in enumerate(results):
            lanes = slice(step * width, (step + 1) * width)
            outs[0][:, lanes] = placed(result.astype(F32), step).astype(BF16)
        return
    send_ref, keep_ref = outs
    half = send_ref.shape[0]
    chosen = chosen_rows(mine, rows, half // 2)
    for step, result in enumerate(results):
        lanes = slice(step * width, (step + 1) * width)
        picked = placed(nn(chosen, result), step)
        sent = picked[0:half]
        send_ref[:, lanes] = (sent if step == 0 else swapped_quarters(sent)).astype(BF16)
        keep_ref[:, lanes] = picked[half:].astype(BF16)


def ordered(weights):
    own, kw2, vw2, far, far2 = weights
    quarter = kw2.shape[0]
    keys = [own[0:quarter], kw2, far[0:quarter], far2[0:quarter]]
    return keys + [own[quarter:], vw2, far[quarter:], far2[quarter:]]


def term_kernel(at, cuts, keep_ref, got_ref, wq_ref, wq2_ref, *refs):
    weights, outs = refs[: -len(cuts)], refs[-len(cuts) :]
    width = wq_ref.shape[1]
    padded = keep_ref.shape[0] // 2
    part = slice(at * padded, (at + 1) * padded)
    keep, got = keep_ref[part, 0:width], got_ref[part, 0:width]
    both = keep_ref[part, width:].astype(F32) + got_ref[part, width:].astype(F32)
    both = both.astype(BF16)
    for (start, stop), out_ref in zip(cuts, outs):
        mine = out_ref.shape[0]
        cut = (stop - start) // 2
        for k in range(2):
            cols = slice(start + k * cut, start + (k + 1) * cut)
            total = nt(keep, wq_ref[cols, :]) + nt(got, wq2_ref[cols, :])
            stacked = jnp.concatenate(ordered([w[:, cols] for w in weights]), axis=0)
            total = total + nn(both, stacked)
            out_ref[:, k * cut : (k + 1) * cut] = total[0:mine, :].astype(out_ref.dtype)


def add_kernel(*refs):
    count = (len(refs) - 1) // 2
    stays, arrivals, out_ref = refs[:count], refs[count:-1], refs[-1]
    at = 0
    for stay, arrived in zip(stays, arrivals):
        cols = slice(at, at + stay.shape[1])
        out_ref[:, cols] = (stay[...] + arrived[...].astype(F32)).astype(BF16)
        at += stay.shape[1]


def per_device(
    norm_out, out_grad, attn_out, log_norm, query_weight, key_weight, value_weight, span_order
):
    shards = lax.axis_size("ctx")
    heads = lax.axis_size("head")
    rows = norm_out.shape[0]
    width = query_weight.shape[1]

    def sent(array, axis, to):
        return lax.ppermute(array, axis, [(i, to(i)) for i in range(lax.axis_size(axis))])

    def flipped(array, axis, bit):
        return sent(array, axis, lambda i: i ^ bit)

    def shifted(array, by):
        return sent(array, "ctx", lambda i: (i + by) % shards)

    kw, vw = key_weight.T, value_weight.T
    quarter, depth = kw.shape
    kw2, vw2 = flipped(kw, "head", 1), flipped(vw, "head", 1)
    wq2 = flipped(query_weight, "head", 1)
    tall = rows + EXTRA
    norm, wkv, grad, attn, lse = local(
        load_kernel,
        (
            ((rows, depth), BF16),
            ((2 * quarter, depth), BF16),
            ((rows, width), BF16),
            ((rows, width), BF16),
            ((1, rows), F32),
        ),
        (norm_out, kw, vw, out_grad, attn_out, log_norm),
        [pltpu.HBM] * 6,
        [pltpu.SemaphoreType.DMA((7,))],
    )
    wkv3 = flipped(wkv, "head", 2)
    keyval = local(keyval_kernel, [((rows, width), BF16)], (norm, wkv, kw2, vw2))
    near_kv = flipped(keyval, "ctx", 1)
    side, far = local(
        query_kernel,
        (((tall, 2 * width), BF16), ((tall, 2 * width), BF16)),
        (norm, query_weight, grad, attn, lse, keyval),
    )
    near = flipped(side, "ctx", 1)
    far = sent(far, "ctx", lambda i: (i + (3 if i % 2 else -3)) % shards)
    pair_kv = local(stack_kernel, [((2 * rows, width), BF16)], (keyval, near_kv))
    kva2 = shifted(pair_kv, 2)
    pair_side = local(stack_kernel, [((2 * tall, 2 * width), BF16)], (side, near))
    later = shifted(pair_side, -2)
    kva1 = local(third_kernel, [((2 * rows, width), BF16)], (keyval, near_kv, far))
    kvx1 = flipped(kva1, "head", 2)
    kvx2 = flipped(kva2, "head", 2)
    wkv4 = flipped(wkv3, "head", 1)
    weights = (wkv, kw2, vw2, wkv3, wkv4)
    fast = heads == GROUP
    mine = rows // heads if fast else None
    tall = 2 * (-(-rows // heads // 8) * 8)
    outs = (((tall, 3 * width), BF16),) * 2 if fast else [((rows, 3 * width), BF16)]
    grads = local(
        functools.partial(attention_kernel, mine),
        outs,
        (span_order, side, near, far, later, kva1, kvx1, kva2, kvx2),
        [pltpu.SMEM] + [pltpu.VMEM] * 8,
    )
    if not fast:
        full = nt(grads[:, :width], query_weight)
        full = full + nn(grads[:, width:], jnp.concatenate(ordered(weights), axis=0))
        return lax.psum_scatter(full.astype(BF16), "head", scatter_dimension=0, tiled=True)
    send, keep = grads
    got = flipped(send, "head", 1)
    operands = (keep, got, query_weight, wq2) + weights
    half = depth // 2
    halves = ((0, half), (half, depth))
    arrived = []
    for cut in halves:
        away = local(functools.partial(term_kernel, 0, (cut,)), [((mine, half), BF16)], operands)
        arrived.append(flipped(away, "head", 2))
    stays = local(
        functools.partial(term_kernel, 1, halves),
        (((mine, half), F32), ((mine, half), F32)),
        operands,
    )
    return local(add_kernel, [((mine, depth), BF16)], tuple(stays) + tuple(arrived))


def solution(mesh):
    in_specs = (
        P("ctx", None),
        P("ctx", "head"),
        P("ctx", "head"),
        P("head", "ctx"),
        P(None, "head"),
        P(None, "head"),
        P(None, "head"),
        P(),
    )
    out_specs = P(("ctx", "head"), None)

    return jax.shard_map(
        per_device, mesh=mesh, in_specs=in_specs, out_specs=out_specs, check_vma=False
    )
```
